1024 devices in a mesh: dp: 8 (over y), ctx: 64 (over z, x), tensor: 2 (over core).
Axes of the slice: x: 4, y: 8, z: 16, core: 2. Of those that a mesh axis runs over, the one named last changes fastest.
Arguments:
- x_seq: bfloat16 [8, 8192, 2048], P('dp', 'ctx', 'tensor'), may hold values from -6 to 6
- dt_seq: float32 [8, 32, 8192], P('dp', 'tensor', 'ctx'), may hold values from 0.05 to 0.5
- b_seq: bfloat16 [8, 8192, 128], P('dp', 'ctx'), may hold values from -2 to 2
- c_seq: bfloat16 [8, 8192, 128], P('dp', 'ctx'), may hold values from -2 to 2
- dy_seq: bfloat16 [8, 8192, 2048], P('dp', 'ctx', 'tensor'), may hold values from -6 to 6
- saved_states: float32 [8, 64, 2048, 128], P('dp', 'ctx', 'tensor'), may hold values from -4 to 4
- doc_starts: int32 [8, 8192], P('dp', 'ctx'), may hold values 0 or 1
- decay_rates: float32 [32], P('tensor'), may hold values from 0.0005 to 0.2
Outputs:
- grad_x: bfloat16 [8, 8192, 2048], P('dp', 'ctx', 'tensor')
- grad_dt: float32 [8, 32, 8192], P('dp', 'tensor', 'ctx')
- grad_b: float32 [8, 8192, 128], P('dp', 'ctx')
- grad_c: float32 [8, 8192, 128], P('dp', 'ctx')
- grad_rates: float32 [8, 32], P('dp', 'tensor')
The draws below stay inside these ranges and needn't reach their ends.
Inputs may be any that keep to these rules, and one draw needn't show every extreme that they name: `doc_starts`: 1 marks the first position of a document; the state restarts there.
All inputs are finite; a program needn't handle non-finite values. No bound on the sum of `doc_starts` on one device may be relied on, other than what follows from the above.
Results may differ from the reference program's by a relative error of at most 0.001.
Values sent between devices are 32-bit elements; how exact they have to be, the bound alone decides.
No kernel may reach another device: no remote copies, remote signals or barrier semaphores. Data moves between devices by JAX's collectives and lax.ppermute only.
A program may use at most 128 MiB of HBM per device.

```python
import math
import jax
import jax.numpy as jnp
from jax import lax

H = 32
P_SIZE = 64
N = 128
TOK_DEV = 128
BLK = 64
DOC_MEAN = 2048
SEQS = 8
LEN = 8192
HP = 2048
N_CTX = 64


def place_ends(array, own_key, least, high):
    place = [jax.random.randint(jax.random.fold_in(own_key, axis), (), 0, length) for axis, length in enumerate(array.shape)]
    longest = array.shape.index(max(array.shape))
    next_to = place[:longest] + [(place[longest] + 1) % array.shape[longest]] + place[longest + 1:]
    return array.at[tuple(place)].set(least).at[tuple(next_to)].set(high)


def shard_levels(stream_key, dims, cuts, low, high):
    loudness = 1.0
    for dim, blocks in cuts:
        steps = jax.random.uniform(jax.random.fold_in(jax.random.fold_in(stream_key, 6), dim), (blocks,), jnp.float32, low / len(cuts), high / len(cuts))
        loudness = loudness * jnp.repeat(jnp.exp(steps), dims[dim] // blocks).reshape((-1,) + (1,) * (len(dims) - 1 - dim))
    return loudness


def centred(stream_key, shape, deviation, reach, cuts=(), kind=jnp.bfloat16):
    array = deviation * jax.random.normal(stream_key, shape, jnp.float32)
    if cuts:
        array = array * shard_levels(stream_key, shape, cuts, -0.22, 0.18)
    return jnp.clip(array, -reach, reach).astype(kind)


def setup_inputs(seed: int = 0) -> dict:
    arg_keys = jax.random.split(jax.random.key(seed), 9)
    x_seq = centred(arg_keys[0], (SEQS, LEN, HP), 1.0, 6.0, ((0, 8), (1, 64), (2, 2)))
    dt_seq = jnp.clip(jnp.exp(math.log(0.5) - 2.3025851 * jax.random.uniform(arg_keys[1], (SEQS, H, LEN), jnp.float32) ** shard_levels(arg_keys[1], (SEQS, H, LEN), ((0, 8), (1, 2), (2, 64)), -0.2, 0.2)), 0.05, 0.5)
    b_seq = centred(arg_keys[2], (SEQS, LEN, N), 0.3, 2.0, ((0, 8), (1, 64)))
    c_seq = centred(arg_keys[3], (SEQS, LEN, N), 0.3, 2.0, ((0, 8), (1, 64)))
    dy_seq = centred(arg_keys[4], (SEQS, LEN, HP), 1.0, 6.0, ((0, 8), (1, 64), (2, 2)))
    saved_states = centred(arg_keys[5], (SEQS, N_CTX, HP, N), 0.5, 4.0, ((0, 8), (1, 64), (2, 2)), jnp.float32)
    doc_starts = place_ends((jax.random.randint(arg_keys[6], (SEQS, LEN), 0, DOC_MEAN) < 1).astype(jnp.int32), jax.random.fold_in(arg_keys[6], 1), 0, 1)
    decay_rates = jnp.clip(jnp.exp(math.log(0.2) - 5.9914645 * jax.random.uniform(arg_keys[7], (H,), jnp.float32) ** shard_levels(arg_keys[7], (H,), ((0, 2),), -0.2, 0.2)), 0.0005, 0.2)
    return {"x_seq": x_seq, "dt_seq": dt_seq, "b_seq": b_seq, "c_seq": c_seq, "dy_seq": dy_seq, "saved_states": saved_states, "doc_starts": doc_starts, "decay_rates": decay_rates}


HIGHEST_PREC = lax.Precision.HIGHEST


def edge_parts(dt_blk, start_blk, rates_blk):
    log_step = -dt_blk * rates_blk[:, None]
    log_cum = jnp.cumsum(log_step, axis=1)
    doc_count = jnp.cumsum(start_blk, axis=0)
    entry_dec = jnp.where(doc_count[None, :] == 0, jnp.exp(log_cum), 0.0)
    tail_dec = jnp.where(doc_count[None, :] == doc_count[-1], jnp.exp(log_cum[:, -1:] - log_cum), 0.0)
    return log_cum, doc_count, entry_dec, tail_dec


def decay_parts(dt_blk, start_blk, rates_blk):
    log_cum, doc_count, entry_dec, tail_dec = edge_parts(dt_blk, start_blk, rates_blk)
    block_len = start_blk.shape[0]
    row_idx = lax.broadcasted_iota(jnp.int32, (block_len, block_len), 0)
    col_idx = lax.broadcasted_iota(jnp.int32, (block_len, block_len), 1)
    below = row_idx >= col_idx
    same_doc = below & (doc_count[:, None] == doc_count[None, :])
    spread = jnp.where(same_doc[None], log_cum[:, :, None] - log_cum[:, None, :], -1e30)
    decay_mat = jnp.exp(spread)
    lower_tri = below.astype(dt_blk.dtype)
    return decay_mat, entry_dec, tail_dec, lower_tri


def advance(x_blk, dt_blk, b_blk, start_blk, rates_blk, h_init):
    _, _, entry_dec, tail_dec = edge_parts(dt_blk, start_blk, rates_blk)
    step_in = dt_blk[:, :, None] * x_blk
    return entry_dec[:, -1][:, None, None] * h_init + jnp.einsum('hs,hsp,sn->hpn', tail_dec, step_in, b_blk, precision=HIGHEST_PREC)


def block_grads(x_blk, dt_blk, b_blk, c_blk, dy_blk, start_blk, rates_blk, h_init, incoming):
    decay_mat, entry_dec, tail_dec, lower_tri = decay_parts(dt_blk, start_blk, rates_blk)
    last_dec = entry_dec[:, -1]
    step_in = dt_blk[:, :, None] * x_blk
    c_dot_b = jnp.dot(c_blk, b_blk.T, precision=HIGHEST_PREC)
    dy_dot_s = jnp.einsum('hup,hsp->hus', dy_blk, step_in, precision=HIGHEST_PREC)
    weight_mat = decay_mat * dy_dot_s
    dy_state = jnp.einsum('htp,hpn->htn', dy_blk, h_init, precision=HIGHEST_PREC)
    grad_cpart = jnp.einsum('hts,sn->tn', weight_mat, b_blk, precision=HIGHEST_PREC) + jnp.einsum('ht,htn->tn', entry_dec, dy_state, precision=HIGHEST_PREC)
    mix_mat = decay_mat * c_dot_b[None]
    f_dot_b = jnp.einsum('tn,hpn->htp', b_blk, incoming, precision=HIGHEST_PREC)
    grad_s = jnp.einsum('hut,hup->htp', mix_mat, dy_blk, precision=HIGHEST_PREC) + tail_dec[:, :, None] * f_dot_b
    s_dot_f = jnp.einsum('htp,hpn->htn', step_in, incoming, precision=HIGHEST_PREC)
    grad_bpart = jnp.einsum('hut,un->tn', weight_mat, c_blk, precision=HIGHEST_PREC) + jnp.einsum('ht,htn->tn', tail_dec, s_dot_f, precision=HIGHEST_PREC)
    kernel_mat = weight_mat * c_dot_b[None]
    prefix_mat = jnp.einsum('hus,ts->hut', kernel_mat, lower_tri, precision=HIGHEST_PREC)
    first_term = jnp.sum(lower_tri[None] * prefix_mat, axis=1)
    q_term = jnp.sum(dy_state * c_blk[None], axis=2)
    second_term = jnp.einsum('hu,ut->ht', entry_dec * q_term, lower_tri, precision=HIGHEST_PREC)
    p_term = jnp.sum(step_in * f_dot_b, axis=2)
    third_term = jnp.einsum('hs,ts->ht', tail_dec * p_term, lower_tri, precision=HIGHEST_PREC)
    fourth_term = last_dec * jnp.sum(incoming * h_init, axis=(1, 2))
    summed = first_term + second_term + third_term + fourth_term[:, None]
    scaled = summed - jnp.sum(grad_s * step_in, axis=2)
    grad_dtpart = jnp.sum(x_blk * grad_s, axis=2) - rates_blk[:, None] * scaled
    grad_xpart = dt_blk[:, :, None] * grad_s
    grad_rpart = -jnp.sum(dt_blk * scaled, axis=1)
    outgoing = jnp.einsum('hu,hup,un->hpn', entry_dec, dy_blk, c_blk, precision=HIGHEST_PREC) + last_dec[:, None, None] * incoming
    return grad_xpart, grad_dtpart, grad_bpart, grad_cpart, grad_rpart, outgoing


def split_blocks(x_loc, dt_loc, b_loc, c_loc, dy_loc, start_loc):
    tok_count, num_heads, head_dim = x_loc.shape
    num_blocks = tok_count // BLK
    x_parts = x_loc.reshape(num_blocks, BLK, num_heads, head_dim).transpose(0, 2, 1, 3)
    dy_parts = dy_loc.reshape(num_blocks, BLK, num_heads, head_dim).transpose(0, 2, 1, 3)
    dt_parts = dt_loc.reshape(num_heads, num_blocks, BLK).transpose(1, 0, 2)
    b_parts = b_loc.reshape(num_blocks, BLK, b_loc.shape[1])
    c_parts = c_loc.reshape(num_blocks, BLK, c_loc.shape[1])
    st_parts = start_loc.reshape(num_blocks, BLK)
    return x_parts, dt_parts, b_parts, c_parts, dy_parts, st_parts


def device_grads(x_loc, dt_loc, b_loc, c_loc, dy_loc, start_loc, rates_loc, h_first, incoming):
    x_parts, dt_parts, b_parts, c_parts, dy_parts, st_parts = split_blocks(x_loc, dt_loc, b_loc, c_loc, dy_loc, start_loc)

    def forward(h_now, pieces):
        x_one, dt_one, b_one, st_one = pieces
        return advance(x_one, dt_one, b_one, st_one, rates_loc, h_now), h_now

    _, h_starts = lax.scan(forward, h_first, (x_parts, dt_parts, b_parts, st_parts))

    def backward(carried, pieces):
        x_one, dt_one, b_one, c_one, dy_one, st_one, h_one = pieces
        results = block_grads(x_one, dt_one, b_one, c_one, dy_one, st_one, rates_loc, h_one, carried)
        return results[5], results[:5]

    final, grads = lax.scan(backward, incoming, (x_parts, dt_parts, b_parts, c_parts, dy_parts, st_parts, h_starts), reverse=True)
    dx_parts, ddt_parts, db_parts, dc_parts, dr_parts = grads
    dx_local = dx_parts.transpose(0, 2, 1, 3).reshape(x_loc.shape)
    ddt_local = ddt_parts.transpose(1, 0, 2).reshape(dt_loc.shape)
    db_local = db_parts.reshape(b_loc.shape)
    dc_local = dc_parts.reshape(c_loc.shape)
    return dx_local, ddt_local, db_local, dc_local, jnp.sum(dr_parts, axis=0), final


def reference(x_seq, dt_seq, b_seq, c_seq, dy_seq, saved_states, doc_starts, decay_rates):
    def one_sequence(pieces):
        x_one, dt_one, b_one, c_one, dy_one, st_one, saved_one = pieces
        x_blocks = x_one.astype(jnp.float32).reshape(N_CTX, TOK_DEV, H, P_SIZE)
        dy_blocks = dy_one.astype(jnp.float32).reshape(N_CTX, TOK_DEV, H, P_SIZE)
        dt_blocks = dt_one.reshape(H, N_CTX, TOK_DEV).transpose(1, 0, 2)
        b_blocks = b_one.astype(jnp.float32).reshape(N_CTX, TOK_DEV, N)
        c_blocks = c_one.astype(jnp.float32).reshape(N_CTX, TOK_DEV, N)
        st_blocks = st_one.reshape(N_CTX, TOK_DEV)
        h_blocks = saved_one.reshape(N_CTX, H, P_SIZE, N)

        def step_back(carried, blocks):
            x_blk, dt_blk, b_blk, c_blk, dy_blk, st_blk, h_blk = blocks
            results = device_grads(x_blk, dt_blk, b_blk, c_blk, dy_blk, st_blk, decay_rates, h_blk, carried)
            return results[5], results[:5]

        _, outputs = lax.scan(step_back, jnp.zeros((H, P_SIZE, N), jnp.float32), (x_blocks, dt_blocks, b_blocks, c_blocks, dy_blocks, st_blocks, h_blocks), reverse=True)
        dx_all, ddt_all, db_all, dc_all, dr_all = outputs
        return (dx_all.reshape(LEN, H * P_SIZE).astype(jnp.bfloat16), ddt_all.transpose(1, 0, 2).reshape(H, LEN), db_all.reshape(LEN, N), dc_all.reshape(LEN, N), jnp.sum(dr_all, axis=0))

    results = lax.map(one_sequence, (x_seq, dt_seq, b_seq, c_seq, dy_seq, doc_starts, saved_states))
    return (results[0], results[1], results[2], results[3], results[4])
```

```python
import jax
import jax.numpy as jnp
from jax import lax
from jax.experimental import pallas as pl
from jax.experimental.pallas import tpu as pltpu
from jax.sharding import Mesh, PartitionSpec as P

F32 = jnp.float32
BF16 = jnp.bfloat16
LANES = 128
HIGHEST = lax.Precision.HIGHEST
INTERPRET = False


def mm(a, b):
    return lax.dot_general(a, b, (((1,), (0,)), ((), ())), preferred_element_type=F32)


def mmt(a, b):
    return lax.dot_general(a, b, (((1,), (1,)), ((), ())), preferred_element_type=F32)


def mm_exact(a, b):
    return lax.dot_general(
        a, b, (((1,), (0,)), ((), ())), precision=HIGHEST, preferred_element_type=F32
    )


def mmt_exact(a, b):
    return lax.dot_general(
        a, b, (((1,), (1,)), ((), ())), precision=HIGHEST, preferred_element_type=F32
    )


def split2(a):
    hi = a.astype(BF16)
    return hi, (a - hi.astype(F32)).astype(BF16)


def split3(a):
    hi = a.astype(BF16)
    rest = a - hi.astype(F32)
    mid = rest.astype(BF16)
    return hi, mid, (rest - mid.astype(F32)).astype(BF16)


def iota(shape, dim):
    return lax.broadcasted_iota(jnp.int32, shape, dim)


def head_rows(rows, width, head_dim):
    return (iota((rows, width), 0) == iota((rows, width), 1) // head_dim).astype(BF16)


def expand(per_head, width, head_dim):
    hot = head_rows(LANES, width, head_dim)
    hi, mid, low = split3(per_head)
    return mm(hi, hot) + mm(mid, hot) + mm(low, hot)


def decays(dt, rates, start):
    heads, tok = dt.shape
    log_step = -dt * rates
    log_step = jnp.concatenate([log_step, jnp.zeros((LANES - heads, tok), F32)], axis=0)
    lower = (iota((tok, tok), 0) >= iota((tok, tok), 1)).astype(F32)
    log_cum = mmt_exact(lower, log_step)
    starts = jnp.broadcast_to(start.astype(F32), (tok, tok))
    docs_down = mmt(lower.astype(BF16), starts.astype(BF16))
    return log_cum, docs_down, starts


def acc_kernel(dy_ref, dt_ref, c_ref, st_ref, rates_ref, out_ref):
    tok, width = dy_ref.shape
    heads = dt_ref.shape[0]
    slices, rows, _ = out_ref.shape
    log_cum, docs, _ = decays(dt_ref[...], rates_ref[...], st_ref[...])
    entry = jnp.where(docs == 0.0, jnp.exp(log_cum), 0.0)
    wide = expand(entry, width, width // heads)
    hi, low = split2(dy_ref[...].astype(F32) * wide)
    eye = (iota((LANES, LANES), 0) == iota((LANES, LANES), 1)).astype(BF16)
    c_t = mmt(eye, c_ref[...]).astype(BF16)
    acc = mm(c_t, hi) + mm(c_t, low)
    last = jnp.broadcast_to(entry[tok - 1 : tok, :], (rows, LANES))
    for i in range(slices):
        out_ref[i, :, :width] = acc[i * rows : (i + 1) * rows, :]
        out_ref[i, :, width:] = last


def local_kernel(
    x_ref,
    dy_ref,
    dt_ref,
    b_ref,
    c_ref,
    h_ref,
    st_ref,
    rates_ref,
    a1_ref,
    a2_ref,
    tx_hi_ref,
    tx_low_ref,
    ht_ref,
    gb_ref,
    gc_ref,
    z_ref,
    q_ref,
    dec_ref,
):
    tok, width = dy_ref.shape
    heads = dt_ref.shape[0]
    head_dim = width // heads
    dt = dt_ref[...]
    log_cum, docs, starts = decays(dt, rates_ref[...], st_ref[...])
    row = iota((tok, tok), 0)
    col = iota((tok, tok), 1)
    upper = (row <= col).astype(BF16)
    docs_across = mm(starts.astype(BF16), upper)
    same = docs == docs_across
    mask = jnp.where(same & (row >= col), 1.0, 0.0)
    mask_t = jnp.where(same & (row <= col), 1.0, 0.0)
    eye = (row == col).astype(F32)
    dt_pad = jnp.concatenate([dt, jnp.zeros((LANES - heads, tok), F32)], axis=0)
    dt_down = mmt_exact(eye, dt_pad)
    growth = jnp.exp(log_cum)
    e_wide = expand(growth, width, head_dim)
    s_wide = expand(jnp.exp(-log_cum) * dt_down, width, head_dim)
    first = jnp.where(docs == 0.0, 1.0, 0.0)
    tail = jnp.where(docs == docs[tok - 1 : tok, :], 1.0, 0.0)
    times = width // LANES
    first_wide = jnp.concatenate([first] * times, axis=1)
    tail_wide = jnp.concatenate([tail] * times, axis=1)
    to_end = s_wide * e_wide[tok - 1 : tok, :] * tail_wide
    x = x_ref[...].astype(F32)
    ey = dy_ref[...].astype(F32) * e_wide
    xs = x * s_wide
    a2_ref[...] = to_end
    tx_hi, tx_low = split2(x * to_end)
    tx_hi_ref[...] = tx_hi
    tx_low_ref[...] = tx_low
    ey_hi, ey_low = split2(ey)
    xs_hi, xs_low = split2(xs)
    h = h_ref[...]
    h_hi, h_low = split2(h)
    ht_ref[...] = h.T
    b = b_ref[...]
    c = c_ref[...]

    weight = mask * (mmt(ey_hi, xs_hi) + mmt(ey_hi, xs_low) + mmt(ey_low, xs_hi))
    w_hi, w_low = split2(weight)
    wt_hi, wt_low = split2(weight.T)
    zero = jnp.zeros((), BF16)
    keep = first_wide > 0.5
    f_hi = jnp.where(keep, ey_hi, zero)
    f_low = jnp.where(keep, ey_low, zero)
    gc_ref[...] = mm(w_hi, b) + mm(w_low, b) + mm(f_hi, h_hi) + mm(f_hi, h_low) + mm(f_low, h_hi)
    gb_ref[...] = mm(wt_hi, c) + mm(wt_low, c)

    g_hi, g_low = split2(mask * mmt(c, b))
    gt_hi, gt_low = split2(mask_t * mmt(b, c))
    a1_ref[...] = s_wide * (mm(gt_hi, ey_hi) + mm(gt_hi, ey_low) + mm(gt_low, ey_hi))
    from_h = first_wide * (mmt(c, h_hi) + mmt(c, h_low))
    y = mm(g_hi, xs_hi) + mm(g_hi, xs_low) + mm(g_low, xs_hi) + from_h
    hot = head_rows(heads, width, head_dim)
    z_hi, z_low = split2(ey * y)
    z_ref[...] = mmt(hot, z_hi) + mmt(hot, z_low)
    q_hi, q_low = split2(ey * from_h)
    q = jnp.sum(mmt(hot, q_hi) + mmt(hot, q_low), axis=1, keepdims=True)
    q_ref[...] = jnp.broadcast_to(q, (heads, tok))
    total = jnp.sum(dt, axis=1, keepdims=True)
    none = jnp.max(starts[:1, :], axis=1, keepdims=True) < 0.5
    dec = jnp.where(none, jnp.exp(-rates_ref[...] * total), 0.0)
    dec_ref[...] = jnp.broadcast_to(dec, (heads, tok))


def total_kernel(got_ref, out_ref, *, width, head_dim):
    members, rows, _ = got_ref.shape
    dec = jnp.concatenate([got_ref[k, :1, width:] for k in range(members)], axis=0)
    wide = expand(dec, width, head_dim)
    carry = got_ref[members - 1, :, :width]
    whole = dec[members - 1 : members, :]
    for k in range(members - 2, -1, -1):
        carry = got_ref[k, :, :width] + wide[k : k + 1, :] * carry
        whole = whole * dec[k : k + 1, :]
    for i in range(out_ref.shape[0]):
        out_ref[i, :, :width] = carry
        out_ref[i, :, width:] = jnp.broadcast_to(whole, (rows, LANES))


def carry_kernel(me_ref, got_ref, totals_ref, out_ref, *, width, head_dim):
    members, rows, _ = got_ref.shape
    groups = totals_ref.shape[0]
    me = me_ref[0]
    dec = jnp.concatenate([totals_ref[k, :1, width:] for k in range(groups)], axis=0)
    dec = jnp.concatenate([dec, jnp.zeros((8 - groups % 8, LANES), F32)], axis=0)
    wide = expand(dec, width, head_dim)
    carry = jnp.zeros((rows, width), F32)
    for k in range(groups - 1, 0, -1):
        new = totals_ref[k, :, :width] + wide[k : k + 1, :] * carry
        carry = jnp.where(k > me, new, carry)
    dec = jnp.concatenate([got_ref[k, :1, width:] for k in range(members)], axis=0)
    wide = expand(dec, width, head_dim)
    for k in range(members - 1, -1, -1):
        out_ref[k, :, :] = carry
        if k:
            carry = got_ref[k, :, :width] + wide[k : k + 1, :] * carry


def final_kernel(
    f_ref,
    x_ref,
    dt_ref,
    b_ref,
    rates_ref,
    a1_ref,
    a2_ref,
    tx_hi_ref,
    tx_low_ref,
    ht_ref,
    gb_ref,
    z_ref,
    q_ref,
    dec_ref,
    gx_ref,
    gdt_ref,
    gb_out_ref,
    dr_ref,
):
    tok, width = x_ref.shape
    heads = dt_ref.shape[0]
    f = jnp.concatenate([f_ref[k] for k in range(f_ref.shape[0])], axis=0)
    f_hi, f_low = split2(f)
    b = b_ref[...]
    gx = a1_ref[...] + a2_ref[...] * (mm(b, f_hi) + mm(b, f_low))
    gx_ref[...] = gx.astype(BF16)
    tx_hi = tx_hi_ref[...]
    gb_out_ref[...] = (
        gb_ref[...] + mmt(tx_hi, f_hi) + mmt(tx_hi, f_low) + mmt(tx_low_ref[...], f_hi)
    )
    hot = head_rows(heads, width, width // heads)
    s_hi, s_low = split2(x_ref[...].astype(F32) * gx)
    ds_s = mmt(hot, s_hi) + mmt(hot, s_low)
    p_hi, p_low = split2(f * ht_ref[...])
    f_h = jnp.sum(mmt(hot, p_hi) + mmt(hot, p_low), axis=1, keepdims=True)
    before = (iota((tok, tok), 0) < iota((tok, tok), 1)).astype(F32)
    r = mm_exact(ds_s - z_ref[...], before) + (q_ref[...] + dec_ref[...] * f_h)
    dt = dt_ref[...]
    gdt_ref[...] = ds_s / dt - rates_ref[...] * r
    dr = -jnp.sum(dt * r, axis=1, keepdims=True)
    dr_ref[...] = jnp.broadcast_to(dr, (heads, LANES))


def call(kernel, outs, *args, scalars=0):
    vmem = pl.BlockSpec(memory_space=pltpu.VMEM)
    smem = pl.BlockSpec(memory_space=pltpu.SMEM)
    return pl.pallas_call(
        kernel,
        out_shape=[jax.ShapeDtypeStruct(s, d) for s, d in outs],
        in_specs=[smem] * scalars + [vmem] * (len(args) - scalars),
        out_specs=[vmem] * len(outs),
        interpret=INTERPRET,
    )(*args)


def per_device(x_seq, dt_seq, b_seq, c_seq, dy_seq, saved_states, doc_starts, decay_rates):
    heads = decay_rates.shape[0]
    tok, width = x_seq.shape[1:]
    head_dim = width // heads
    n = b_seq.shape[2]
    groups = lax.axis_size("zo")
    near = lax.axis_size("zi") * lax.axis_size("cx")
    rows = n // near
    x, dt, b, c, dy = (a[0] for a in (x_seq, dt_seq, b_seq, c_seq, dy_seq))
    h = saved_states[0, 0]
    rates = decay_rates[:, None]
    (acc,) = call(acc_kernel, [((near, rows, width + LANES), F32)], dy, dt, c, doc_starts, rates)
    got = lax.all_to_all(acc, ("zi", "cx"), 0, 0)
    wide, small, square = (tok, width), (heads, tok), (tok, n)
    a1, a2, tx_hi, tx_low, ht, gb, gc, z, q, dec = call(
        local_kernel,
        [
            (wide, F32),
            (wide, F32),
            (wide, BF16),
            (wide, BF16),
            ((n, width), F32),
            (square, F32),
            (square, F32),
            (small, F32),
            (small, F32),
            (small, F32),
        ],
        *(x, dy, dt, b, c, h, doc_starts, rates),
    )
    swap = [(0, 1), (1, 0)]
    gc_sum = gc + lax.ppermute(gc, "tensor", swap)

    def totals(got_ref, out_ref):
        total_kernel(got_ref, out_ref, width=width, head_dim=head_dim)

    (total,) = call(totals, [((groups, rows, width + LANES), F32)], got)
    spread = lax.all_to_all(total, "zo", 0, 0)

    def carries(me_ref, got_ref, totals_ref, out_ref):
        carry_kernel(me_ref, got_ref, totals_ref, out_ref, width=width, head_dim=head_dim)

    me = lax.axis_index("zo").astype(jnp.int32).reshape(1)
    (carry,) = call(carries, [((near, rows, width), F32)], me, got, spread, scalars=1)
    incoming = lax.all_to_all(carry, ("zi", "cx"), 0, 0)
    gx, gdt, gb_all, dr = call(
        final_kernel,
        [(wide, BF16), (small, F32), (square, F32), ((heads, LANES), F32)],
        *(incoming, x, dt, b, rates, a1, a2, tx_hi, tx_low, ht, gb, z, q, dec),
    )
    gb_sum = gb_all + lax.ppermute(gb_all, "tensor", swap)
    ctx = groups * near
    dr_all = jnp.broadcast_to(dr[:, 0].reshape(1, 1, heads), (ctx, 1, heads))
    dr_sum = jnp.sum(lax.all_to_all(dr_all, ("zo", "zi", "cx"), 0, 0), axis=0)
    return gx[None], gdt[None], gb_sum[None], gc_sum[None], dr_sum


def solution(mesh):
    sizes = dict(mesh.shape)
    dp, ctx, tensor = sizes["dp"], sizes["ctx"], sizes["tensor"]
    inner = 4 if ctx % 64 == 0 else 2
    names = ("dp", "zo", "zi", "cx", "tensor")
    split = Mesh(mesh.devices.reshape(dp, ctx // inner**2, inner, inner, tensor), names)
    ctx_axes = ("zo", "zi", "cx")
    return jax.shard_map(
        per_device,
        mesh=split,
        in_specs=(
            P("dp", ctx_axes, "tensor"),
            P("dp", "tensor", ctx_axes),
            P("dp", ctx_axes, None),
            P("dp", ctx_axes, None),
            P("dp", ctx_axes, "tensor"),
            P("dp", ctx_axes, "tensor", None),
            P("dp", ctx_axes),
            P("tensor"),
        ),
        out_specs=(
            P("dp", ctx_axes, "tensor"),
            P("dp", "tensor", ctx_axes),
            P("dp", ctx_axes, None),
            P("dp", ctx_axes, None),
            P("dp", "tensor"),
        ),
        check_vma=False,
    )
```

```python
import jax
import jax.numpy as jnp
from jax import lax
from jax.experimental import pallas as pl
from jax.experimental.pallas import tpu as pltpu
from jax.sharding import Mesh, PartitionSpec as P

F32 = jnp.float32
BF16 = jnp.bfloat16
LANES = 128
HIGHEST = lax.Precision.HIGHEST
INTERPRET = False


def mm(a, b):
    return lax.dot_general(a, b, (((1,), (0,)), ((), ())), preferred_element_type=F32)


def mmt(a, b):
    return lax.dot_general(a, b, (((1,), (1,)), ((), ())), preferred_element_type=F32)


def mm_exact(a, b):
    return lax.dot_general(
        a, b, (((1,), (0,)), ((), ())), precision=HIGHEST, preferred_element_type=F32
    )


def mmt_exact(a, b):
    return lax.dot_general(
        a, b, (((1,), (1,)), ((), ())), precision=HIGHEST, preferred_element_type=F32
    )


def split2(a):
    hi = a.astype(BF16)
    return hi, (a - hi.astype(F32)).astype(BF16)


def split3(a):
    hi = a.astype(BF16)
    rest = a - hi.astype(F32)
    mid = rest.astype(BF16)
    return hi, mid, (rest - mid.astype(F32)).astype(BF16)


def iota(shape, dim):
    return lax.broadcasted_iota(jnp.int32, shape, dim)


def head_rows(rows, width, head_dim):
    return (iota((rows, width), 0) == iota((rows, width), 1) // head_dim).astype(BF16)


def expand(per_head, width, head_dim):
    hot = head_rows(LANES, width, head_dim)
    hi, mid, low = split3(per_head)
    return mm(hi, hot) + mm(mid, hot) + mm(low, hot)


def decays(dt, rates, start):
    heads, tok = dt.shape
    dt = jnp.concatenate([dt, jnp.zeros((LANES - heads, tok), F32)], axis=0)
    lower = (iota((tok, tok), 0) >= iota((tok, tok), 1)).astype(F32)
    rates = jnp.concatenate([rates, jnp.zeros((1, LANES - heads), F32)], axis=1)
    log_cum = -rates * mmt_exact(lower, dt)
    starts = jnp.broadcast_to(start.astype(F32), (tok, tok))
    docs_down = mmt(lower.astype(BF16), starts.astype(BF16))
    return log_cum, docs_down, starts


def acc_kernel(dy_ref, dt_ref, c_ref, st_ref, rates_ref, out_ref):
    tok, width = dy_ref.shape
    heads = dt_ref.shape[0]
    slices, rows, _ = out_ref.shape
    log_cum, docs, _ = decays(dt_ref[...], rates_ref[...], st_ref[...])
    entry = jnp.where(docs == 0.0, jnp.exp(log_cum), 0.0)
    wide = expand(entry, width, width // heads)
    hi, low = split2(dy_ref[...].astype(F32) * wide)
    eye = (iota((LANES, LANES), 0) == iota((LANES, LANES), 1)).astype(BF16)
    c_t = mmt(eye, c_ref[...]).astype(BF16)
    acc = mm(c_t, hi) + mm(c_t, low)
    last = jnp.broadcast_to(entry[tok - 1 : tok, :], (rows, LANES))
    for i in range(slices):
        out_ref[i, :, :width] = acc[i * rows : (i + 1) * rows, :]
        out_ref[i, :, width:] = last


def local_kernel(
    x_ref,
    dy_ref,
    dt_ref,
    b_ref,
    c_ref,
    h_ref,
    st_ref,
    rates_ref,
    a1_ref,
    a2_ref,
    tx_hi_ref,
    tx_low_ref,
    ht_ref,
    gb_ref,
    gc_ref,
    z_ref,
    q_ref,
    dec_ref,
    lam_ref,
    mt_ref,
    dr_ref,
):
    tok, width = dy_ref.shape
    heads = dt_ref.shape[0]
    head_dim = width // heads
    dt = dt_ref[...]
    log_cum, docs, starts = decays(dt, rates_ref[...], st_ref[...])
    row = iota((tok, tok), 0)
    col = iota((tok, tok), 1)
    upper = (row <= col).astype(BF16)
    docs_across = mm(starts.astype(BF16), upper)
    same = docs == docs_across
    mask = jnp.where(same & (row >= col), 1.0, 0.0)
    mask_t = jnp.where(same & (row <= col), 1.0, 0.0)
    eye = (row == col).astype(F32)
    dt_pad = jnp.concatenate([dt, jnp.zeros((LANES - heads, tok), F32)], axis=0)
    dt_down = mmt_exact(eye, dt_pad)
    growth = jnp.exp(log_cum)
    e_wide = expand(growth, width, head_dim)
    s_wide = expand(jnp.exp(-log_cum) * dt_down, width, head_dim)
    first = jnp.where(docs == 0.0, 1.0, 0.0)
    tail = jnp.where(docs == docs[tok - 1 : tok, :], 1.0, 0.0)
    times = width // LANES
    first_wide = jnp.concatenate([first] * times, axis=1)
    tail_wide = jnp.concatenate([tail] * times, axis=1)
    to_end = s_wide * e_wide[tok - 1 : tok, :] * tail_wide
    x = x_ref[...].astype(F32)
    ey = dy_ref[...].astype(F32) * e_wide
    xs = x * s_wide
    a2_ref[...] = to_end
    tx_hi, tx_low = split2(x * to_end)
    tx_hi_ref[...] = tx_hi
    tx_low_ref[...] = tx_low
    ey_hi, ey_low = split2(ey)
    xs_hi, xs_low = split2(xs)
    h = h_ref[...]
    h_hi, h_low = split2(h)
    ht = h.T
    ht_ref[...] = ht
    b = b_ref[...]
    c = c_ref[...]

    weight = mask * (mmt(ey_hi, xs_hi) + mmt(ey_hi, xs_low) + mmt(ey_low, xs_hi))
    w_hi, w_low = split2(weight)
    wt_hi, wt_low = split2(weight.T)
    zero = jnp.zeros((), BF16)
    keep = first_wide > 0.5
    f_hi = jnp.where(keep, ey_hi, zero)
    f_low = jnp.where(keep, ey_low, zero)
    gc_ref[...] = mm(w_hi, b) + mm(w_low, b) + mm(f_hi, h_hi) + mm(f_hi, h_low) + mm(f_low, h_hi)
    gb_ref[...] = mm(wt_hi, c) + mm(wt_low, c)

    g_hi, g_low = split2(mask * mmt(c, b))
    gt_hi, gt_low = split2(mask_t * mmt(b, c))
    a1 = s_wide * (mm(gt_hi, ey_hi) + mm(gt_hi, ey_low) + mm(gt_low, ey_hi))
    a1_ref[...] = a1
    from_h = first_wide * (mmt(c, h_hi) + mmt(c, h_low))
    y = mm(g_hi, xs_hi) + mm(g_hi, xs_low) + mm(g_low, xs_hi) + from_h
    hot = head_rows(heads, width, head_dim)
    z_hi, z_low = split2(ey * y)
    z = mmt(hot, z_hi) + mmt(hot, z_low)
    z_ref[...] = z
    q_hi, q_low = split2(ey * from_h)
    q = jnp.sum(mmt(hot, q_hi) + mmt(hot, q_low), axis=1, keepdims=True)
    q_ref[...] = jnp.broadcast_to(q, (heads, tok))
    rates = jnp.concatenate([rates_ref[...], jnp.zeros((1, LANES - heads), F32)], axis=1)
    diag = iota((heads, LANES), 0) == iota((heads, LANES), 1)
    lam = mmt_exact(jnp.where(diag, rates, 0.0), jnp.ones((tok, LANES), F32))
    lam_ref[...] = lam
    total = jnp.sum(dt, axis=1, keepdims=True)
    none = jnp.max(starts[:1, :], axis=1, keepdims=True) < 0.5
    dec_ref[...] = jnp.where(none, jnp.exp(-lam * total), 0.0)

    s_hi, s_low = split2(x * a1)
    before = (row < col).astype(F32)
    r = mm_exact(mmt(hot, s_hi) + mmt(hot, s_low) - z, before) + q
    local = -jnp.sum(dt * r, axis=1, keepdims=True)
    dr_ref[...] = jnp.sum(jnp.where(diag, local, 0.0), axis=0, keepdims=True)
    later_wide = expand(mmt_exact(before, dt_pad), width, head_dim)
    b_t = mmt(eye.astype(BF16), b).astype(BF16)
    m_hi, m_low = split2(x * to_end * later_wide)
    all_dt = jnp.sum(dt_down, axis=0, keepdims=True)
    last = jnp.where(docs[tok - 1 :, :] == 0.0, growth[tok - 1 :, :] * all_dt, 0.0)
    mt_ref[...] = mm(b_t, m_hi) + mm(b_t, m_low) + ht * expand(last, width, head_dim)


def rates_kernel(f_ref, mt_ref, dr_ref, out_ref, *, head_dim):
    n, width = mt_ref.shape
    ctx = out_ref.shape[0]
    rows = f_ref.shape[1]
    part = f_ref[0] * mt_ref[:rows, :]
    for k in range(1, n // rows):
        part = part + f_ref[k] * mt_ref[k * rows : (k + 1) * rows, :]
    hot = head_rows(LANES, width, head_dim)
    each = mmt_exact(part, hot.astype(F32))
    out = dr_ref[...] - jnp.sum(each, axis=0, keepdims=True)
    out_ref[...] = jnp.broadcast_to(out.reshape(1, 1, LANES), (ctx, 1, LANES))


def total_kernel(got_ref, out_ref, *, width, head_dim):
    members, rows, _ = got_ref.shape
    dec = jnp.concatenate([got_ref[k, :1, width:] for k in range(members)], axis=0)
    wide = expand(dec, width, head_dim)
    carry = got_ref[members - 1, :, :width]
    whole = dec[members - 1 : members, :]
    for k in range(members - 2, -1, -1):
        carry = got_ref[k, :, :width] + wide[k : k + 1, :] * carry
        whole = whole * dec[k : k + 1, :]
    for i in range(out_ref.shape[0]):
        out_ref[i, :, :width] = carry
        out_ref[i, :, width:] = jnp.broadcast_to(whole, (rows, LANES))


def carry_kernel(me_ref, got_ref, totals_ref, out_ref, *, width, head_dim):
    members, rows, _ = got_ref.shape
    groups = totals_ref.shape[0]
    me = me_ref[0]
    dec = jnp.concatenate([totals_ref[k, :1, width:] for k in range(groups)], axis=0)
    dec = jnp.concatenate([dec, jnp.zeros((8 - groups % 8, LANES), F32)], axis=0)
    wide = expand(dec, width, head_dim)
    carry = jnp.zeros((rows, width), F32)
    for k in range(groups - 1, 0, -1):
        new = totals_ref[k, :, :width] + wide[k : k + 1, :] * carry
        carry = jnp.where(k > me, new, carry)
    dec = jnp.concatenate([got_ref[k, :1, width:] for k in range(members)], axis=0)
    wide = expand(dec, width, head_dim)
    for k in range(members - 1, -1, -1):
        out_ref[k, :, :] = carry
        if k:
            carry = got_ref[k, :, :width] + wide[k : k + 1, :] * carry


def final_kernel(
    f_ref,
    x_ref,
    dt_ref,
    b_ref,
    a1_ref,
    a2_ref,
    tx_hi_ref,
    tx_low_ref,
    ht_ref,
    gb_ref,
    z_ref,
    q_ref,
    dec_ref,
    lam_ref,
    after_ref,
    gx_ref,
    gdt_ref,
    gb_out_ref,
):
    del after_ref
    tok, width = x_ref.shape
    heads = dt_ref.shape[0]
    f = jnp.concatenate([f_ref[k] for k in range(f_ref.shape[0])], axis=0)
    f_hi, f_low = split2(f)
    b = b_ref[...]
    gx = a1_ref[...] + a2_ref[...] * (mm(b, f_hi) + mm(b, f_low))
    gx_ref[...] = gx.astype(BF16)
    tx_hi = tx_hi_ref[...]
    gb_out_ref[...] = (
        gb_ref[...] + mmt(tx_hi, f_hi) + mmt(tx_hi, f_low) + mmt(tx_low_ref[...], f_hi)
    )
    hot = head_rows(heads, width, width // heads)
    s_hi, s_low = split2(x_ref[...].astype(F32) * gx)
    ds_s = mmt(hot, s_hi) + mmt(hot, s_low)
    p_hi, p_low = split2(f * ht_ref[...])
    f_h = jnp.sum(mmt(hot, p_hi) + mmt(hot, p_low), axis=1, keepdims=True)
    before = (iota((tok, tok), 0) < iota((tok, tok), 1)).astype(F32)
    r = mm_exact(ds_s - z_ref[...], before) + (q_ref[...] + dec_ref[...] * f_h)
    gdt_ref[...] = ds_s / dt_ref[...] - lam_ref[...] * r


def call(kernel, outs, *args, scalars=0, near=(), far=(), unread=0, mib=8):
    vmem = pl.BlockSpec(memory_space=pltpu.VMEM)
    smem = pl.BlockSpec(memory_space=pltpu.SMEM)
    if INTERPRET:
        shapes = [jax.ShapeDtypeStruct(s, d) for s, d, *_ in outs]
    else:
        shapes = [(pltpu.HBM if off else pltpu.VMEM)(s, d) for s, d, *off in outs]
        place = {**dict.fromkeys(far, pltpu.HBM), **dict.fromkeys(near, pltpu.VMEM)}
        args = [
            pltpu.with_memory_space_constraint(a, place[i]) if i in place else a
            for i, a in enumerate(args)
        ]
    return pl.pallas_call(
        kernel,
        out_shape=shapes,
        in_specs=[smem] * scalars
        + [vmem] * (len(args) - scalars - unread)
        + [pl.BlockSpec(memory_space=pl.ANY)] * unread,
        out_specs=[vmem] * len(outs),
        compiler_params=pltpu.CompilerParams(vmem_limit_bytes=mib << 20),
        interpret=INTERPRET,
    )(*args)


def per_device(x_seq, dt_seq, b_seq, c_seq, dy_seq, saved_states, doc_starts, decay_rates):
    heads = decay_rates.shape[0]
    tok, width = x_seq.shape[1:]
    head_dim = width // heads
    n = b_seq.shape[2]
    groups = lax.axis_size("zo")
    near = lax.axis_size("zi") * lax.axis_size("cx")
    ctx = groups * near
    rows = n // near
    x, dt, b, c, dy = (a[0] for a in (x_seq, dt_seq, b_seq, c_seq, dy_seq))
    h = saved_states[0, 0]
    rates = decay_rates[None]
    (acc,) = call(acc_kernel, [((near, rows, width + LANES), F32)], dy, dt, c, doc_starts, rates)
    got = lax.all_to_all(acc, ("zi", "cx"), 0, 0)
    wide, small, square, state = (tok, width), (heads, tok), (tok, n), (n, width)
    local = call(
        local_kernel,
        [
            (wide, F32, True),
            (wide, F32, True),
            (wide, BF16, True),
            (wide, BF16, True),
            (state, F32, True),
            (square, F32, True),
            (square, F32),
            (small, F32, True),
            (small, F32, True),
            (small, F32, True),
            (small, F32, True),
            (state, F32),
            ((1, LANES), F32),
        ],
        *(x, dy, dt, b, c, h, doc_starts, rates),
        mib=24,
    )
    a1, a2, tx_hi, tx_low, ht, gb, gc, z, q, dec, lam, mt, dr = local
    swap = [(0, 1), (1, 0)]
    gc_sum = gc + lax.ppermute(gc, "tensor", swap)

    def totals(got_ref, out_ref):
        total_kernel(got_ref, out_ref, width=width, head_dim=head_dim)

    (total,) = call(totals, [((groups, rows, width + LANES), F32)], got, near=(0,))
    spread = lax.all_to_all(total, "zo", 0, 0)

    def carries(me_ref, got_ref, totals_ref, out_ref):
        carry_kernel(me_ref, got_ref, totals_ref, out_ref, width=width, head_dim=head_dim)

    me = lax.axis_index("zo").astype(jnp.int32).reshape(1)
    (carry,) = call(
        carries, [((near, rows, width), F32)], me, got, spread, scalars=1, near=(1, 2)
    )
    incoming = lax.all_to_all(carry, ("zi", "cx"), 0, 0)

    def rates_sum(f_ref, mt_ref, dr_ref, out_ref):
        rates_kernel(f_ref, mt_ref, dr_ref, out_ref, head_dim=head_dim)

    (dr_all,) = call(
        rates_sum, [((ctx, 1, LANES), F32)], incoming, mt, dr, near=(0, 1, 2)
    )
    dr_parts = lax.all_to_all(dr_all, ("zo", "zi", "cx"), 0, 0)
    dr_sum = jnp.sum(dr_parts, axis=0)[:, :heads]
    gx, gdt, gb_all = call(
        final_kernel,
        [(wide, BF16, True), (small, F32, True), (square, F32)],
        *(incoming, x, dt, b, a1, a2, tx_hi, tx_low, ht, gb, z, q, dec, lam, dr_all),
        near=(0,),
        far=range(4, 14),
        unread=1,
        mib=16,
    )
    gb_sum = gb_all + lax.ppermute(gb_all, "tensor", swap)
    return gx[None], gdt[None], gb_sum[None], gc_sum[None], dr_sum


def solution(mesh):
    sizes = dict(mesh.shape)
    dp, ctx, tensor = sizes["dp"], sizes["ctx"], sizes["tensor"]
    inner = 4 if ctx % 64 == 0 else 2
    names = ("dp", "zo", "zi", "cx", "tensor")
    split = Mesh(mesh.devices.reshape(dp, ctx // inner**2, inner, inner, tensor), names)
    ctx_axes = ("zo", "zi", "cx")
    return jax.shard_map(
        per_device,
        mesh=split,
        in_specs=(
            P("dp", ctx_axes, "tensor"),
            P("dp", "tensor", ctx_axes),
            P("dp", ctx_axes, None),
            P("dp", ctx_axes, None),
            P("dp", ctx_axes, "tensor"),
            P("dp", ctx_axes, "tensor", None),
            P("dp", ctx_axes),
            P("tensor"),
        ),
        out_specs=(
            P("dp", ctx_axes, "tensor"),
            P("dp", "tensor", ctx_axes),
            P("dp", ctx_axes, None),
            P("dp", ctx_axes, None),
            P("dp", "tensor"),
        ),
        check_vma=False,
    )
```

```python
import jax
import jax.numpy as jnp
from jax import lax
from jax.experimental import pallas as pl
from jax.experimental.pallas import tpu as pltpu
from jax.sharding import Mesh, PartitionSpec as P

F32 = jnp.float32
BF16 = jnp.bfloat16
LANES = 128
HIGHEST = lax.Precision.HIGHEST
INTERPRET = False


def mm(a, b):
    return lax.dot_general(a, b, (((1,), (0,)), ((), ())), preferred_element_type=F32)


def mmt(a, b):
    return lax.dot_general(a, b, (((1,), (1,)), ((), ())), preferred_element_type=F32)


def mm_exact(a, b):
    return lax.dot_general(
        a, b, (((1,), (0,)), ((), ())), precision=HIGHEST, preferred_element_type=F32
    )


def mmt_exact(a, b):
    return lax.dot_general(
        a, b, (((1,), (1,)), ((), ())), precision=HIGHEST, preferred_element_type=F32
    )


def split2(a):
    hi = a.astype(BF16)
    return hi, (a - hi.astype(F32)).astype(BF16)


def split3(a):
    hi = a.astype(BF16)
    rest = a - hi.astype(F32)
    mid = rest.astype(BF16)
    return hi, mid, (rest - mid.astype(F32)).astype(BF16)


def iota(shape, dim):
    return lax.broadcasted_iota(jnp.int32, shape, dim)


def head_rows(rows, width, head_dim):
    return (iota((rows, width), 0) == iota((rows, width), 1) // head_dim).astype(BF16)


def expand(per_head, width, head_dim):
    hot = head_rows(LANES, width, head_dim)
    hi, mid, low = split3(per_head)
    return mm(hi, hot) + mm(mid, hot) + mm(low, hot)


def decays(dt, rates, start):
    heads, tok = dt.shape
    dt = jnp.concatenate([dt, jnp.zeros((LANES - heads, tok), F32)], axis=0)
    lower = (iota((tok, tok), 0) >= iota((tok, tok), 1)).astype(F32)
    rates = jnp.concatenate([rates, jnp.zeros((1, LANES - heads), F32)], axis=1)
    log_cum = -rates * mmt_exact(lower, dt)
    starts = jnp.broadcast_to(start.astype(F32), (tok, tok))
    docs_down = mmt(lower.astype(BF16), starts.astype(BF16))
    return log_cum, docs_down, starts


def acc_kernel(dy_ref, dt_ref, c_ref, st_ref, rates_ref, out_ref):
    tok, width = dy_ref.shape
    heads = dt_ref.shape[0]
    slices, rows, _ = out_ref.shape
    log_cum, docs, _ = decays(dt_ref[...], rates_ref[...], st_ref[...])
    entry = jnp.where(docs == 0.0, jnp.exp(log_cum), 0.0)
    wide = expand(entry, width, width // heads)
    hi, low = split2(dy_ref[...].astype(F32) * wide)
    eye = (iota((LANES, LANES), 0) == iota((LANES, LANES), 1)).astype(BF16)
    c_t = mmt(eye, c_ref[...]).astype(BF16)
    acc = mm(c_t, hi) + mm(c_t, low)
    last = jnp.broadcast_to(entry[tok - 1 : tok, :], (rows, LANES))
    for i in range(slices):
        out_ref[i, :, :width] = acc[i * rows : (i + 1) * rows, :]
        out_ref[i, :, width:] = last


def local_kernel(
    x_ref,
    dy_ref,
    dt_ref,
    b_ref,
    c_ref,
    h_ref,
    st_ref,
    rates_ref,
    a1_ref,
    a2_ref,
    tx_hi_ref,
    tx_low_ref,
    ht_ref,
    gb_ref,
    gc_ref,
    z_ref,
    q_ref,
    dec_ref,
    lam_ref,
    mt_ref,
    dr_ref,
):
    tok, width = dy_ref.shape
    heads = dt_ref.shape[0]
    head_dim = width // heads
    dt = dt_ref[...]
    log_cum, docs, starts = decays(dt, rates_ref[...], st_ref[...])
    row = iota((tok, tok), 0)
    col = iota((tok, tok), 1)
    upper = (row <= col).astype(BF16)
    docs_across = mm(starts.astype(BF16), upper)
    same = docs == docs_across
    mask = jnp.where(same & (row >= col), 1.0, 0.0)
    mask_t = jnp.where(same & (row <= col), 1.0, 0.0)
    eye = (row == col).astype(F32)
    dt_pad = jnp.concatenate([dt, jnp.zeros((LANES - heads, tok), F32)], axis=0)
    dt_down = mmt_exact(eye, dt_pad)
    growth = jnp.exp(log_cum)
    e_wide = expand(growth, width, head_dim)
    s_wide = expand(jnp.exp(-log_cum) * dt_down, width, head_dim)
    first = jnp.where(docs == 0.0, 1.0, 0.0)
    tail = jnp.where(docs == docs[tok - 1 : tok, :], 1.0, 0.0)
    times = width // LANES
    first_wide = jnp.concatenate([first] * times, axis=1)
    tail_wide = jnp.concatenate([tail] * times, axis=1)
    to_end = s_wide * e_wide[tok - 1 : tok, :] * tail_wide
    x = x_ref[...].astype(F32)
    ey = dy_ref[...].astype(F32) * e_wide
    xs = x * s_wide
    a2_ref[...] = to_end
    tx_hi, tx_low = split2(x * to_end)
    tx_hi_ref[...] = tx_hi
    tx_low_ref[...] = tx_low
    ey_hi, ey_low = split2(ey)
    xs_hi, xs_low = split2(xs)
    h = h_ref[...]
    h_hi, h_low = split2(h)
    ht = h.T
    ht_ref[...] = ht
    b = b_ref[...]
    c = c_ref[...]

    weight = mask * (mmt(ey_hi, xs_hi) + mmt(ey_hi, xs_low) + mmt(ey_low, xs_hi))
    w_hi, w_low = split2(weight)
    wt_hi, wt_low = split2(weight.T)
    zero = jnp.zeros((), BF16)
    keep = first_wide > 0.5
    f_hi = jnp.where(keep, ey_hi, zero)
    f_low = jnp.where(keep, ey_low, zero)
    gc_ref[...] = mm(w_hi, b) + mm(w_low, b) + mm(f_hi, h_hi) + mm(f_hi, h_low) + mm(f_low, h_hi)
    gb_ref[...] = mm(wt_hi, c) + mm(wt_low, c)

    g_hi, g_low = split2(mask * mmt(c, b))
    gt_hi, gt_low = split2(mask_t * mmt(b, c))
    a1 = s_wide * (mm(gt_hi, ey_hi) + mm(gt_hi, ey_low) + mm(gt_low, ey_hi))
    a1_ref[...] = a1
    from_h = first_wide * (mmt(c, h_hi) + mmt(c, h_low))
    y = mm(g_hi, xs_hi) + mm(g_hi, xs_low) + mm(g_low, xs_hi) + from_h
    hot = head_rows(heads, width, head_dim)
    z_hi, z_low = split2(ey * y)
    z = mmt(hot, z_hi) + mmt(hot, z_low)
    z_ref[...] = z
    q_hi, q_low = split2(ey * from_h)
    q = jnp.sum(mmt(hot, q_hi) + mmt(hot, q_low), axis=1, keepdims=True)
    q_ref[...] = jnp.broadcast_to(q, (heads, tok))
    rates = jnp.concatenate([rates_ref[...], jnp.zeros((1, LANES - heads), F32)], axis=1)
    diag = iota((heads, LANES), 0) == iota((heads, LANES), 1)
    lam = mmt_exact(jnp.where(diag, rates, 0.0), jnp.ones((tok, LANES), F32))
    lam_ref[...] = lam
    total = jnp.sum(dt, axis=1, keepdims=True)
    none = jnp.max(starts[:1, :], axis=1, keepdims=True) < 0.5
    dec_ref[...] = jnp.where(none, jnp.exp(-lam * total), 0.0)

    s_hi, s_low = split2(x * a1)
    before = (row < col).astype(F32)
    r = mm_exact(mmt(hot, s_hi) + mmt(hot, s_low) - z, before) + q
    local = -jnp.sum(dt * r, axis=1, keepdims=True)
    dr_ref[...] = jnp.sum(jnp.where(diag, local, 0.0), axis=0, keepdims=True)
    later_wide = expand(mmt_exact(before, dt_pad), width, head_dim)
    b_t = mmt(eye.astype(BF16), b).astype(BF16)
    m_hi, m_low = split2(x * to_end * later_wide)
    all_dt = jnp.sum(dt_down, axis=0, keepdims=True)
    last = jnp.where(docs[tok - 1 :, :] == 0.0, growth[tok - 1 :, :] * all_dt, 0.0)
    mt_ref[...] = mm(b_t, m_hi) + mm(b_t, m_low) + ht * expand(last, width, head_dim)


def rates_kernel(f_ref, mt_ref, dr_ref, out_ref, *, head_dim):
    n, width = mt_ref.shape
    ctx = out_ref.shape[0]
    rows = f_ref.shape[1]
    part = f_ref[0] * mt_ref[:rows, :]
    for k in range(1, n // rows):
        part = part + f_ref[k] * mt_ref[k * rows : (k + 1) * rows, :]
    heads = width // head_dim
    hot = head_rows(heads, width, head_dim)
    each = jnp.sum(mmt_exact(hot.astype(F32), part), axis=1, keepdims=True)
    diag = iota((heads, LANES), 0) == iota((heads, LANES), 1)
    out = dr_ref[...] - jnp.sum(jnp.where(diag, each, 0.0), axis=0, keepdims=True)
    out_ref[...] = jnp.broadcast_to(out.reshape(1, 1, LANES), (ctx, 1, LANES))


def total_kernel(got_ref, out_ref, *, width, head_dim):
    members, rows, _ = got_ref.shape
    dec = jnp.concatenate([got_ref[k, :1, width:] for k in range(members)], axis=0)
    wide = expand(dec, width, head_dim)
    carry = got_ref[members - 1, :, :width]
    whole = dec[members - 1 : members, :]
    for k in range(members - 2, -1, -1):
        carry = got_ref[k, :, :width] + wide[k : k + 1, :] * carry
        whole = whole * dec[k : k + 1, :]
    for i in range(out_ref.shape[0]):
        out_ref[i, :, :width] = carry
        out_ref[i, :, width:] = jnp.broadcast_to(whole, (rows, LANES))


def carry_kernel(me_ref, got_ref, totals_ref, out_ref, *, width, head_dim):
    members, rows, _ = got_ref.shape
    groups = totals_ref.shape[0]
    me = me_ref[0]
    dec = jnp.concatenate([totals_ref[k, :1, width:] for k in range(groups)], axis=0)
    dec = jnp.concatenate([dec, jnp.zeros((8 - groups % 8, LANES), F32)], axis=0)
    wide = expand(dec, width, head_dim)
    carry = jnp.zeros((rows, width), F32)
    for k in range(groups - 1, 0, -1):
        new = totals_ref[k, :, :width] + wide[k : k + 1, :] * carry
        carry = jnp.where(k > me, new, carry)
    dec = jnp.concatenate([got_ref[k, :1, width:] for k in range(members)], axis=0)
    wide = expand(dec, width, head_dim)
    for k in range(members - 1, -1, -1):
        out_ref[k, :, :] = carry
        if k:
            carry = got_ref[k, :, :width] + wide[k : k + 1, :] * carry


def final_kernel(
    f_ref,
    x_ref,
    dt_ref,
    b_ref,
    a1_ref,
    a2_ref,
    tx_hi_ref,
    tx_low_ref,
    ht_ref,
    gb_ref,
    z_ref,
    q_ref,
    dec_ref,
    lam_ref,
    after_ref,
    gx_ref,
    gdt_ref,
    gb_out_ref,
):
    del after_ref
    tok, width = x_ref.shape
    heads = dt_ref.shape[0]
    f = jnp.concatenate([f_ref[k] for k in range(f_ref.shape[0])], axis=0)
    f_hi, f_low = split2(f)
    b = b_ref[...]
    gx = a1_ref[...] + a2_ref[...] * (mm(b, f_hi) + mm(b, f_low))
    gx_ref[...] = gx.astype(BF16)
    tx_hi = tx_hi_ref[...]
    gb_out_ref[...] = (
        gb_ref[...] + mmt(tx_hi, f_hi) + mmt(tx_hi, f_low) + mmt(tx_low_ref[...], f_hi)
    )
    hot = head_rows(heads, width, width // heads)
    s_hi, s_low = split2(x_ref[...].astype(F32) * gx)
    ds_s = mmt(hot, s_hi) + mmt(hot, s_low)
    p_hi, p_low = split2(f * ht_ref[...])
    f_h = jnp.sum(mmt(hot, p_hi) + mmt(hot, p_low), axis=1, keepdims=True)
    before = (iota((tok, tok), 0) < iota((tok, tok), 1)).astype(F32)
    r = mm_exact(ds_s - z_ref[...], before) + (q_ref[...] + dec_ref[...] * f_h)
    gdt_ref[...] = ds_s / dt_ref[...] - lam_ref[...] * r


def call(kernel, outs, *args, scalars=0, near=(), far=(), unread=0, mib=8):
    vmem = pl.BlockSpec(memory_space=pltpu.VMEM)
    smem = pl.BlockSpec(memory_space=pltpu.SMEM)
    if INTERPRET:
        shapes = [jax.ShapeDtypeStruct(s, d) for s, d, *_ in outs]
    else:
        shapes = [(pltpu.HBM if off else pltpu.VMEM)(s, d) for s, d, *off in outs]
        place = {**dict.fromkeys(far, pltpu.HBM), **dict.fromkeys(near, pltpu.VMEM)}
        args = [
            pltpu.with_memory_space_constraint(a, place[i]) if i in place else a
            for i, a in enumerate(args)
        ]
    return pl.pallas_call(
        kernel,
        out_shape=shapes,
        in_specs=[smem] * scalars
        + [vmem] * (len(args) - scalars - unread)
        + [pl.BlockSpec(memory_space=pl.ANY)] * unread,
        out_specs=[vmem] * len(outs),
        compiler_params=pltpu.CompilerParams(vmem_limit_bytes=mib << 20),
        interpret=INTERPRET,
    )(*args)


def per_device(x_seq, dt_seq, b_seq, c_seq, dy_seq, saved_states, doc_starts, decay_rates):
    heads = decay_rates.shape[0]
    tok, width = x_seq.shape[1:]
    head_dim = width // heads
    n = b_seq.shape[2]
    groups = lax.axis_size("zo")
    near = lax.axis_size("zi") * lax.axis_size("cx")
    ctx = groups * near
    rows = n // near
    x, dt, b, c, dy = (a[0] for a in (x_seq, dt_seq, b_seq, c_seq, dy_seq))
    h = saved_states[0, 0]
    rates = decay_rates[None]
    (acc,) = call(
        acc_kernel,
        [((near, rows, width + LANES), F32)],
        *(dy, dt, c, doc_starts, rates),
        far=range(5),
    )
    got = lax.all_to_all(acc, ("zi", "cx"), 0, 0)
    wide, small, square, state = (tok, width), (heads, tok), (tok, n), (n, width)
    local = call(
        local_kernel,
        [
            (wide, F32, True),
            (wide, F32, True),
            (wide, BF16, True),
            (wide, BF16, True),
            (state, F32, True),
            (square, F32, True),
            (square, F32),
            (small, F32, True),
            (small, F32, True),
            (small, F32, True),
            (small, F32, True),
            (state, F32),
            ((1, LANES), F32),
        ],
        *(x, dy, dt, b, c, h, doc_starts, rates),
        mib=24,
    )
    a1, a2, tx_hi, tx_low, ht, gb, gc, z, q, dec, lam, mt, dr = local
    swap = [(0, 1), (1, 0)]
    gc_sum = gc + lax.ppermute(gc, "tensor", swap)

    def totals(got_ref, out_ref):
        total_kernel(got_ref, out_ref, width=width, head_dim=head_dim)

    (total,) = call(totals, [((groups, rows, width + LANES), F32)], got, near=(0,))
    spread = lax.all_to_all(total, "zo", 0, 0)

    def carries(me_ref, got_ref, totals_ref, out_ref):
        carry_kernel(me_ref, got_ref, totals_ref, out_ref, width=width, head_dim=head_dim)

    me = lax.axis_index("zo").astype(jnp.int32).reshape(1)
    (carry,) = call(
        carries, [((near, rows, width), F32)], me, got, spread, scalars=1, near=(1, 2)
    )
    incoming = lax.all_to_all(carry, ("zi", "cx"), 0, 0)

    def rates_sum(f_ref, mt_ref, dr_ref, out_ref):
        rates_kernel(f_ref, mt_ref, dr_ref, out_ref, head_dim=head_dim)

    (dr_all,) = call(
        rates_sum, [((ctx, 1, LANES), F32)], incoming, mt, dr, near=(0, 1, 2)
    )
    dr_parts = lax.all_to_all(dr_all, ("zo", "zi", "cx"), 0, 0)
    dr_sum = jnp.sum(dr_parts, axis=0)[:, :heads]
    gx, gdt, gb_all = call(
        final_kernel,
        [(wide, BF16, True), (small, F32, True), (square, F32)],
        *(incoming, x, dt, b, a1, a2, tx_hi, tx_low, ht, gb, z, q, dec, lam, dr_all),
        near=(0,),
        far=range(4, 14),
        unread=1,
        mib=16,
    )
    gb_sum = gb_all + lax.ppermute(gb_all, "tensor", swap)
    return gx[None], gdt[None], gb_sum[None], gc_sum[None], dr_sum


def solution(mesh):
    sizes = dict(mesh.shape)
    dp, ctx, tensor = sizes["dp"], sizes["ctx"], sizes["tensor"]
    inner = 4 if ctx % 64 == 0 else 2
    names = ("dp", "zo", "zi", "cx", "tensor")
    split = Mesh(mesh.devices.reshape(dp, ctx // inner**2, inner, inner, tensor), names)
    ctx_axes = ("zo", "zi", "cx")
    return jax.shard_map(
        per_device,
        mesh=split,
        in_specs=(
            P("dp", ctx_axes, "tensor"),
            P("dp", "tensor", ctx_axes),
            P("dp", ctx_axes, None),
            P("dp", ctx_axes, None),
            P("dp", ctx_axes, "tensor"),
            P("dp", ctx_axes, "tensor", None),
            P("dp", ctx_axes),
            P("tensor"),
        ),
        out_specs=(
            P("dp", ctx_axes, "tensor"),
            P("dp", "tensor", ctx_axes),
            P("dp", ctx_axes, None),
            P("dp", ctx_axes, None),
            P("dp", "tensor"),
        ),
        check_vma=False,
    )
```
